512 devices in a mesh: section: 32 (over y_hi, z, core), expert: 16 (over y_lo, x).
Axes of the slice: x: 4, y: 8 (y_hi: 2, y_lo: 4; y = y_hi * 4 + y_lo), z: 8, core: 2. Of those that a mesh axis runs over, the one named last changes fastest.
Arguments:
- acts: bfloat16 [32, 2048, 2048], P('section', 'expert'), may hold values from -6 to 6
- routes: int32 [32, 2048, 2], P('section', 'expert'), may hold values from 0 to 3, all different within a row; in each aligned block of 128 rows (0 to 127, 128 to 255, ..., all dimensions but the last counted through in order) at most 96 rows name the same one
- gates: float32 [32, 2048, 2], P('section', 'expert'), may hold values from 0.2 to 1
- norm_gain: float32 [32, 2048], P('section'), may hold values from 0.5 to 1.5
- gate_w: bfloat16 [32, 2048, 4096], P('section', None, 'expert'), may hold values from -0.125 to 0.125
- up_w: bfloat16 [32, 2048, 4096], P('section', None, 'expert'), may hold values from -0.125 to 0.125
- down_w: bfloat16 [32, 4096, 2048], P('section', 'expert'), may hold values from -0.1875 to 0.1875
Outputs:
- result: bfloat16 [32, 2048, 2048], P('section', 'expert')
The draws below stay inside these ranges and needn't reach their ends.
Inputs may be any that keep to these rules, and one draw needn't show every extreme that they name: `routes`: each token names 2 different experts. Among the rows of one device, no expert is named by more than 96 tokens, and in every draw some expert is named by exactly 96.
All inputs are finite; a program needn't handle non-finite values.
Results may differ from the reference program's by a relative error of at most 0.005.
Values may be sent and summed in bfloat16 or wider, within the bound.
A program may use at most 64 MiB of HBM per device.

```python
import math
import jax
import jax.numpy as jnp
import numpy as np
from jax import lax

D = 2048
HID = 1024
NEXP = 4
TOPK = 2
TOK_DEV = 128
CAP = 96
TOK_SECTION = 2048
N_SECTION = 32
N_EXPERT = 16


def levels(rng, extent, split, low, top_value):
    loudness, own = 1.0, jax.random.fold_in(rng, 6)
    for axis_at, blocks in split:
        steps = jnp.exp(jax.random.uniform(jax.random.fold_in(own, axis_at), (blocks,), jnp.float32, low / len(split), top_value / len(split)))
        loudness = loudness * jnp.repeat(steps, extent[axis_at] // blocks).reshape([-1 if axis == axis_at else 1 for axis in range(len(extent))])
    return loudness


def assign_block(key, own, number, rows, count, top, most, lean):
    sequence = jax.random.permutation(key, count)
    heavy_load, common = load_shares(count, rows * top, most, lean, True), load_shares(count, rows * top, most, lean, False)
    places = jnp.arange(count)

    def named(lengths, rotation):
        used = int((lengths > 0).sum())
        fixed = max(1, used // 4)
        passed = fixed + (places - fixed + rotation * (used - fixed)) % max(1, count - fixed)
        return jnp.zeros((count,), jnp.int32).at[sequence[jnp.where(places < fixed, places, passed)]].set(jnp.asarray(lengths, jnp.int32))

    lengths = jnp.where(number % 4 == 0, named(heavy_load, number // 4), named(common, number - number // 4 - 1))
    mixed = jax.random.permutation(jax.random.fold_in(own, 3), count)
    giver, sink = mixed[0:count // 2 * 2:2], mixed[1:count // 2 * 2:2]
    room = jnp.minimum(lengths[giver] - 1, most - lengths[sink]) // 2
    room = jnp.where((giver == sequence[0]) | (sink == sequence[0]) | (lengths[sink] == 0), 0, jnp.maximum(room, 0))
    passed = jax.random.randint(jax.random.fold_in(own, 4), (count // 2,), 0, 1 << 20) % (room + 1)
    lengths = lengths.at[giver].add(-passed).at[sink].add(passed)
    items = jnp.searchsorted(jnp.cumsum(lengths), jnp.arange(rows * top), side="right").astype(jnp.int32)
    grid = items.reshape(top, rows).T
    grid = grid[jax.random.permutation(jax.random.fold_in(own, 1), rows)]
    rotation = jax.random.randint(jax.random.fold_in(own, 2), (rows, 1), 0, top)
    return jnp.take_along_axis(grid, (jnp.arange(top)[None, :] + rotation) % top, axis=1)


def load_shares(count, total, most, slope, full):
    portions = [(1 << 20) // math.isqrt(standing ** slope) + 1 for standing in range(1, count + 1)]
    largest = most if full else min(most, max(-(-total // count), total * portions[0] // sum(portions)))
    least = 1 if total - largest >= count - 1 else 0
    given, spare = [largest] + [least] * (count - 1), total - largest - least * (count - 1)
    while spare > 0:
        candidates = [i for i in range(1, count) if given[i] < largest] or [i for i in range(1, count) if given[i] < most]
        mass, left = sum([portions[i] for i in candidates]), spare
        for i in candidates:
            extra = min(most - given[i], max(1, left * portions[i] // mass), spare)
            given[i] = given[i] + extra
            spare = spare - extra
    return np.array(given)


def noise(own_key, shape, scale, reach, cuts=(), kind=jnp.bfloat16):
    array = jax.random.normal(own_key, shape, jnp.float32) * scale
    if len(cuts) > 0:
        array = levels(own_key, shape, cuts, -0.22, 0.18) * array
    return jnp.clip(array, min=-reach, max=reach).astype(kind)


def setup_inputs(seed: int = 0) -> dict:
    splits = jax.random.split(jax.random.key(seed), 8)
    acts = noise(splits[0], (N_SECTION, TOK_SECTION, D), 1.0, 6.0, ((0, 32), (1, 16)))
    routes_keys = jax.random.split(jax.random.fold_in(splits[1], 1), N_SECTION * TOK_SECTION // TOK_DEV)
    routes_turns = jax.random.permutation(jax.random.fold_in(splits[1], 3), N_SECTION * TOK_SECTION // TOK_DEV)
    routes = jax.vmap(lambda own, number: assign_block(jax.random.fold_in(splits[1], 2), own, number, TOK_DEV, NEXP, TOPK, CAP, 2))(routes_keys, routes_turns).reshape((N_SECTION, TOK_SECTION, TOPK))
    gates = jnp.clip(0.2 + 0.8 * jax.random.uniform(splits[2], (N_SECTION, TOK_SECTION, TOPK), jnp.float32) ** levels(splits[2], (N_SECTION, TOK_SECTION, TOPK), ((0, 32), (1, 16)), -0.2, 0.2), 0.2, 1.0)
    norm_gain = jnp.clip(1.0 + 0.1 * jax.random.normal(splits[3], (N_SECTION, D), jnp.float32), 0.5, 1.5)
    gate_w = noise(splits[4], (N_SECTION, D, NEXP * HID), D ** -0.5, 0.125, ((0, 32), (2, 16)))
    up_w = noise(splits[5], (N_SECTION, D, NEXP * HID), D ** -0.5, 0.125, ((0, 32), (2, 16)))
    down_w = noise(splits[6], (N_SECTION, NEXP * HID, D), HID ** -0.5, 0.1875, ((0, 32), (1, 16)))
    return {"acts": acts, "routes": routes, "gates": gates, "norm_gain": norm_gain, "gate_w": gate_w, "up_w": up_w, "down_w": down_w}


def one_section(pack):
    xin, ids, weights, gain, wgate, wup, wdown = pack
    xf = xin.astype(jnp.float32)
    scale = lax.rsqrt(lax.optimization_barrier(jnp.mean(xf * xf, axis=1, keepdims=True)) + 1e-06)
    normed = (xf * scale * gain[None, :]).astype(jnp.bfloat16)
    hsplit = N_EXPERT // NEXP
    width = HID // hsplit
    limit = min(TOK_SECTION, CAP * N_EXPERT)
    total = xf
    for g in range(NEXP):
        chosen = (ids == g).astype(jnp.int32)
        member = lax.optimization_barrier(jnp.sum(chosen, axis=1))
        order = jnp.argsort(1 - member, stable=True)[:limit].astype(jnp.int32)
        rows = normed[order]
        weight_g = lax.optimization_barrier(jnp.sum(weights * chosen.astype(jnp.float32), axis=1))[order]
        expert_out = jnp.zeros((limit, D), jnp.float32)
        for h in range(hsplit):
            first = g * HID + h * width
            gpart = jnp.dot(rows, wgate[:, first:first + width], preferred_element_type=jnp.float32)
            upart = jnp.dot(rows, wup[:, first:first + width], preferred_element_type=jnp.float32)
            hidden = (jax.nn.silu(gpart) * upart).astype(jnp.bfloat16)
            part = jnp.dot(hidden, wdown[first:first + width, :], preferred_element_type=jnp.float32).astype(jnp.bfloat16)
            expert_out = expert_out + part.astype(jnp.float32)
        total = total.at[order].add(weight_g[:, None] * expert_out)
    return total.astype(jnp.bfloat16)

def reference(acts, routes, gates, norm_gain, gate_w, up_w, down_w):
    incoming = jnp.roll(acts, 1, axis=0)
    return lax.map(one_section, (incoming, routes, gates, norm_gain, gate_w, up_w, down_w))
```

```python
import functools

import jax
import jax.numpy as jnp
from jax import lax
from jax.experimental import pallas as pl
from jax.experimental.pallas import tpu as pltpu
from jax.sharding import PartitionSpec as P

NEXP = 4
CAP = 96
SHIFT_PARTS = 4
MESH = pl.DeviceIdType.MESH
F32 = jnp.float32
BF16 = jnp.bfloat16


def far_order(y, k):
    low = y < 2
    yy = jnp.where(low, y, 3 - y)
    d = 3 - k
    d = jnp.where(d <= yy, d - 1, d)
    return jnp.where(low, d, 3 - d)


def kernel(
    acts, routes, gates, gain, gate_w, up_w, down_w, out,
    inc, packs, rows, wg, wu, wd, normed, hidden, own_part, mate_part, got_part,
    summed, back, place_t, place, gate_of,
    shift_s, shift_r, w_s, w_r, w_l, y_s, y_r, rel_s, rel_r, part_s, part_r, ret_s, ret_r,
):
    tok, dim = inc.shape
    width = gate_w.shape[1]
    n_sec = lax.axis_size("section")
    s = lax.axis_index("section")
    e = lax.axis_index("expert")
    core = lax.rem(s, 2)
    x = lax.rem(e, 4)
    y = e // 4
    flip = x + 1 - 2 * lax.rem(x, 2)
    cross = 3 - x
    wx = jnp.where(core == 0, flip, cross)
    tx = jnp.where(core == 0, cross, flip)
    nxt = (lax.rem(s + 1, n_sec), e)
    prv = (lax.rem(s + n_sec - 1, n_sec), e)
    wmate = (s, y * 4 + wx)
    tmate = (s, y * 4 + tx)

    def at_row(r):
        return (s, r * 4 + x)

    barrier = pltpu.get_barrier_semaphore()
    for peer in (nxt, prv, wmate, tmate):
        pl.semaphore_signal(barrier, inc=1, device_id=peer, device_id_type=MESH)
    for i in range(1, 4):
        pl.semaphore_signal(barrier, inc=1, device_id=at_row(lax.rem(y + i, 4)), device_id_type=MESH)

    local = [
        pltpu.make_async_copy(gate_w, wg.at[0], w_l.at[0]),
        pltpu.make_async_copy(up_w, wu.at[0], w_l.at[1]),
        pltpu.make_async_copy(down_w, wd.at[pl.ds(0, width)], w_l.at[2]),
    ]
    for copy in local:
        copy.start()
    pl.semaphore_wait(barrier, 7)

    part = dim // SHIFT_PARTS
    shifts = [
        pltpu.make_async_remote_copy(
            acts.at[:, pl.ds(i * part, part)], inc.at[:, pl.ds(i * part, part)],
            shift_s.at[i], shift_r.at[i], device_id=nxt, device_id_type=MESH)
        for i in range(SHIFT_PARTS)
    ]
    for copy in shifts:
        copy.start()
    weights = [
        pltpu.make_async_remote_copy(src, dst, w_s.at[i], w_r.at[i], device_id=wmate, device_id_type=MESH)
        for i, (src, dst) in enumerate(
            ((gate_w, wg.at[1]), (up_w, wu.at[1]), (down_w, wd.at[pl.ds(width, width)])))
    ]
    for copy in weights:
        copy.start()

    lane = lax.broadcasted_iota(jnp.int32, (tok, tok), 1)
    sub = lax.broadcasted_iota(jnp.int32, (tok, tok), 0)
    first, second = routes[:, 0:1] == lane, routes[:, 1:2] == lane
    member = (first | second).astype(F32)
    gate_of[...] = jnp.where(first, gates[:, 0:1], 0.0) + jnp.where(second, gates[:, 1:2], 0.0)
    tri = (lane <= sub).astype(BF16)
    rank = jnp.dot(tri, member.astype(BF16), preferred_element_type=F32) - 1.0
    slot = lane.astype(F32)
    for g in range(NEXP):
        hot = jnp.where(rank[:, g:g + 1] == slot, member[:, g:g + 1], 0.0)
        place_t[g] = hot.astype(BF16)
        place[g] = hot.T.astype(BF16)

    def packed(g, cols):
        return jnp.dot(place[g][:CAP], inc[:, cols], preferred_element_type=F32).astype(BF16)

    for i in range(SHIFT_PARTS):
        shifts[i].wait_recv()
        cols = pl.ds(i * part, part)
        for k in range(3):
            packs[k, :, cols] = packed(far_order(y, k), cols)
        rows[y, 0, :, cols] = packed(y, cols)

    def dispatch(k):
        return pltpu.make_async_remote_copy(
            packs.at[k], rows.at[y, 0], y_s.at[k], y_r.at[y],
            device_id=at_row(far_order(y, k)), device_id_type=MESH)

    for k in range(3):
        dispatch(k).start()

    def arrival(src):
        return pltpu.make_async_remote_copy(
            packs.at[0], rows.at[src, 0], y_s.at[0], y_r.at[src],
            device_id=at_row(src), device_id_type=MESH)

    def relay(src):
        return pltpu.make_async_remote_copy(
            rows.at[src, 0], rows.at[src, 1], rel_s.at[src], rel_r.at[src],
            device_id=tmate, device_id_type=MESH)

    def norm(src, which):
        xf = rows[src, which].astype(F32)
        scale = lax.rsqrt(jnp.mean(xf * xf, axis=1, keepdims=True) + 1e-06)
        normed[src, pl.ds(which * CAP, CAP), :] = (xf * scale * gain[...]).astype(BF16)

    def activate(src, half):
        xn = normed[src]
        gpart = jnp.dot(xn, wg[half], preferred_element_type=F32)
        upart = jnp.dot(xn, wu[half], preferred_element_type=F32)
        hidden[src, :, pl.ds(half * width, width)] = (jax.nn.silu(gpart) * upart).astype(BF16)

    for copy in local:
        copy.wait()

    @pl.loop(0, 5)
    def _(b):
        @pl.when(b < 4)
        def _():
            src = lax.rem(y + b, 4)

            @pl.when(b > 0)
            def _():
                arrival(src).wait_recv()

            relay(src).start()
            norm(src, 0)

        @pl.when(b > 0)
        def _():
            src = lax.rem(y + b + 3, 4)
            relay(src).wait_recv()
            norm(src, 1)
            activate(src, 0)

    for copy in weights:
        copy.wait_recv()

    def partial(src):
        return pltpu.make_async_remote_copy(
            mate_part.at[src], got_part.at[src], part_s.at[src], part_r.at[src],
            device_id=tmate, device_id_type=MESH)

    def giveback(src):
        return pltpu.make_async_remote_copy(
            summed.at[src], back.at[y], ret_s.at[src], ret_r.at[y],
            device_id=at_row(src), device_id_type=MESH)

    tile = dim // 4

    @pl.loop(0, 5)
    def _(b):
        @pl.when(b < 4)
        def _():
            src = lax.rem(y + b + 1, 4)
            activate(src, 1)
            hid = hidden[src]
            for t in range(4):
                cols = pl.ds(t * tile, tile)
                value = jnp.dot(hid, wd[:, cols], preferred_element_type=F32)
                own_part[src, :, cols] = value[:CAP]
                mate_part[src, :, cols] = value[CAP:].astype(BF16)
            partial(src).start()

        @pl.when(b > 0)
        def _():
            src = lax.rem(y + b, 4)
            partial(src).wait_recv()
            total = (own_part[src] + got_part[src].astype(F32)).astype(BF16)

            @pl.when(b < 4)
            def _():
                summed[src] = total
                giveback(src).start()

            @pl.when(b == 4)
            def _():
                back[y] = total

    for i in range(1, 4):
        g = lax.rem(y + i, 4)
        pltpu.make_async_remote_copy(
            summed.at[0], back.at[g], ret_s.at[0], ret_r.at[g],
            device_id=at_row(g), device_id_type=MESH).wait_recv()

    for t in range(4):
        cols = pl.ds(t * tile, tile)
        total = inc[:, cols].astype(F32)
        for g in range(NEXP):
            total = total + gate_of[:, g:g + 1] * jnp.dot(
                place_t[g][:, :CAP], back[g, :, cols], preferred_element_type=F32)
        out[:, cols] = total.astype(BF16)

    for copy in shifts:
        copy.wait_send()
    for copy in weights:
        copy.wait_send()
    for k in range(3):
        dispatch(k).wait_send()
    for i in range(4):
        relay(i).wait_send()
        partial(i).wait_send()
    for i in range(1, 4):
        giveback(lax.rem(y + i, 4)).wait_send()


def local(acts, routes, gates, norm_gain, gate_w, up_w, down_w):
    tok, dim = acts.shape[1:]
    width = gate_w.shape[2]
    hbm = pl.BlockSpec(memory_space=pl.ANY)
    vmem = pl.BlockSpec(memory_space=pltpu.VMEM)
    dma = pltpu.SemaphoreType.DMA
    both = 2 * CAP
    result = pl.pallas_call(
        kernel,
        name="relay_experts",
        out_shape=jax.ShapeDtypeStruct((tok, dim), BF16),
        in_specs=[hbm, vmem, vmem, vmem, hbm, hbm, hbm],
        out_specs=vmem,
        scratch_shapes=[
            pltpu.VMEM((tok, dim), BF16),
            pltpu.VMEM((3, CAP, dim), BF16),
            pltpu.VMEM((4, 2, CAP, dim), BF16),
            pltpu.VMEM((2, dim, width), BF16),
            pltpu.VMEM((2, dim, width), BF16),
            pltpu.VMEM((2 * width, dim), BF16),
            pltpu.VMEM((4, both, dim), BF16),
            pltpu.VMEM((4, both, 2 * width), BF16),
            pltpu.VMEM((4, CAP, dim), F32),
            pltpu.VMEM((4, CAP, dim), BF16),
            pltpu.VMEM((4, CAP, dim), BF16),
            pltpu.VMEM((4, CAP, dim), BF16),
            pltpu.VMEM((4, CAP, dim), BF16),
            pltpu.VMEM((4, tok, tok), BF16),
            pltpu.VMEM((4, tok, tok), BF16),
            pltpu.VMEM((tok, tok), F32),
            dma((SHIFT_PARTS,)), dma((SHIFT_PARTS,)),
            dma((3,)), dma((3,)), dma((3,)),
            dma((3,)), dma((4,)),
            dma((4,)), dma((4,)),
            dma((4,)), dma((4,)),
            dma((4,)), dma((4,)),
        ],
        compiler_params=pltpu.CompilerParams(
            collective_id=0, has_side_effects=True, vmem_limit_bytes=56 * 1024 * 1024),
    )(acts[0], routes[0], gates[0], norm_gain, gate_w[0], up_w[0], down_w[0])
    return result.reshape(1, tok, dim)


def solution(mesh):
    in_specs = (
        P("section", "expert", None),
        P("section", "expert", None),
        P("section", "expert", None),
        P("section", None),
        P("section", None, "expert"),
        P("section", None, "expert"),
        P("section", "expert", None),
    )
    out_specs = P("section", "expert", None)
    return jax.shard_map(local, mesh=mesh, in_specs=in_specs, out_specs=out_specs, check_vma=False)
```

```python
import functools

import jax
import jax.numpy as jnp
from jax import lax
from jax.experimental import pallas as pl
from jax.experimental.pallas import tpu as pltpu
from jax.sharding import PartitionSpec as P

NEXP = 4
CAP = 96
SHIFT_PARTS = 4
EARLY = 2
MESH = pl.DeviceIdType.MESH
F32 = jnp.float32
BF16 = jnp.bfloat16


def far_order(y, k):
    low = y < 2
    yy = jnp.where(low, y, 3 - y)
    d = 3 - k
    d = jnp.where(d <= yy, d - 1, d)
    return jnp.where(low, d, 3 - d)


def kernel(
    acts, routes, gates, gain, gate_w, up_w, down_w, out,
    inc, hop, packs, rows, wg, wu, wd, normed, hidden, own_part, mate_part, got_part,
    summed, back, place_t, place, gate_of,
    shift_s, shift_r, hop_s, hop_r, w_s, w_r, w_l, y_s, y_r, rel_s, rel_r, part_s, part_r, ret_s, ret_r,
):
    tok, dim = inc.shape
    width = gate_w.shape[1]
    n_sec = lax.axis_size("section")
    half = n_sec // 2
    s = lax.axis_index("section")
    e = lax.axis_index("expert")
    core = lax.rem(s, 2)
    x = lax.rem(e, 4)
    y = e // 4
    flip = x + 1 - 2 * lax.rem(x, 2)
    cross = 3 - x
    wx = jnp.where(core == 0, flip, cross)
    tx = jnp.where(core == 0, cross, flip)
    nxt = (lax.rem(s + 1, n_sec), e)
    prv = (lax.rem(s + n_sec - 1, n_sec), e)
    wmate = (s, y * 4 + wx)
    tmate = (s, y * 4 + tx)
    leaves = lax.rem(s, half) == half - 1
    enters = lax.rem(s, half) == 0
    ring = (s // half) * 4 + y

    def around(steps, last):
        to = lax.rem(ring + 8 + steps, 8)
        return ((to // 4) * half + last * (half - 1), lax.rem(to, 4) * 4 + x)

    def at_row(r):
        return (s, r * 4 + x)

    def greet(peer):
        pl.semaphore_signal(barrier, inc=1, device_id=peer, device_id_type=MESH)

    barrier = pltpu.get_barrier_semaphore()
    greet(wmate)
    greet(tmate)
    for i in range(1, 4):
        greet(at_row(lax.rem(y + i, 4)))

    @pl.when(enters)
    def _():
        for last in range(2):
            greet(around(2, last))
            greet(around(-2, last))

    @pl.when(jnp.logical_not(enters))
    def _():
        greet(prv)

    local = [
        pltpu.make_async_copy(gate_w, wg.at[0], w_l.at[0]),
        pltpu.make_async_copy(up_w, wu.at[0], w_l.at[1]),
        pltpu.make_async_copy(down_w, wd.at[pl.ds(0, width)], w_l.at[2]),
    ]
    for copy in local:
        copy.start()
    pl.semaphore_wait(barrier, 6 + jnp.where(leaves, 1, 0) + jnp.where(enters, 2, 0))

    part = dim // SHIFT_PARTS
    columns = [pl.ds(i * part, part) for i in range(SHIFT_PARTS)]

    def shift(i, peer):
        return pltpu.make_async_remote_copy(
            acts.at[:, columns[i]], inc.at[:, columns[i]],
            shift_s.at[i], shift_r.at[i], device_id=peer, device_id_type=MESH)

    def first_leg(i):
        return pltpu.make_async_remote_copy(
            acts.at[:, columns[i]], hop.at[:, columns[i]], shift_s.at[i], hop_r.at[i],
            device_id=around(2 if i % 2 == 0 else -2, 0), device_id_type=MESH)

    def second_leg(i):
        return pltpu.make_async_remote_copy(
            hop.at[:, columns[i]], inc.at[:, columns[i]], hop_s.at[i], shift_r.at[i],
            device_id=around(2 if i % 2 == 0 else -2, 0), device_id_type=MESH)

    @pl.when(leaves)
    def _():
        for i in range(SHIFT_PARTS):
            first_leg(i).start()

    @pl.when(jnp.logical_not(leaves))
    def _():
        for i in range(SHIFT_PARTS):
            shift(i, nxt).start()

    weights = [
        pltpu.make_async_remote_copy(src, dst, w_s.at[i], w_r.at[i], device_id=wmate, device_id_type=MESH)
        for i, (src, dst) in enumerate(
            ((gate_w, wg.at[1]), (up_w, wu.at[1]), (down_w, wd.at[pl.ds(width, width)])))
    ]
    for copy in weights:
        copy.start()

    lane = lax.broadcasted_iota(jnp.int32, (tok, tok), 1)
    sub = lax.broadcasted_iota(jnp.int32, (tok, tok), 0)
    first, second = routes[0:1, :] == sub, routes[1:2, :] == sub
    member = (first | second).astype(F32)
    gate_of[...] = (jnp.where(first, gates[0:1, :], 0.0) + jnp.where(second, gates[1:2, :], 0.0)).T
    rank = jnp.dot(member.astype(BF16), (sub <= lane).astype(BF16), preferred_element_type=F32) - 1.0
    slot = sub.astype(F32)
    for g in range(NEXP):
        hot = jnp.where(rank[g:g + 1, :] == slot, member[g:g + 1, :], 0.0)
        place[g] = hot.astype(BF16)
        place_t[g] = hot.T.astype(BF16)

    @pl.when(enters)
    def _():
        for i in range(SHIFT_PARTS):
            first_leg(i).wait_recv()
            second_leg(i).start()

    def packed(g, cols):
        return jnp.dot(place[g][:CAP], inc[:, cols], preferred_element_type=F32).astype(BF16)

    for i in range(SHIFT_PARTS):
        shift(i, nxt).wait_recv()
        cols = columns[i]
        for k in range(3):
            packs[k, :, cols] = packed(far_order(y, k), cols)
        rows[0, y, :, cols] = packed(y, cols)

    def dispatch(k):
        return pltpu.make_async_remote_copy(
            packs.at[k], rows.at[0, y], y_s.at[k], y_r.at[y],
            device_id=at_row(far_order(y, k)), device_id_type=MESH)

    for k in range(3):
        dispatch(k).start()

    def arrival(src):
        return pltpu.make_async_remote_copy(
            packs.at[0], rows.at[0, src], y_s.at[0], y_r.at[src],
            device_id=at_row(src), device_id_type=MESH)

    def relay(src):
        return pltpu.make_async_remote_copy(
            rows.at[0, src], rows.at[1, src], rel_s.at[src], rel_r.at[src],
            device_id=tmate, device_id_type=MESH)

    def block(b):
        return jnp.where(b == 3, y, far_order(y, jnp.minimum(b, 2)))

    def norm(which, src):
        xf = rows[which, src].astype(F32)
        scale = lax.rsqrt(jnp.mean(xf * xf, axis=1, keepdims=True) + 1e-06)
        return (xf * scale * gain[...]).astype(BF16)

    def activate(xn, part):
        gpart = jnp.dot(xn, wg[part], preferred_element_type=F32)
        upart = jnp.dot(xn, wu[part], preferred_element_type=F32)
        return (jax.nn.silu(gpart) * upart).astype(BF16)

    normed[y] = norm(0, y)

    @pl.loop(0, 3)
    def _(b):
        src = block(b)
        arrival(src).wait_recv()

        @pl.when(b < EARLY)
        def _():
            relay(src).start()

        normed[src] = norm(0, src)

    for b in range(3, EARLY):
        relay(block(b)).start()

    for copy in local:
        copy.wait()

    def own_rows(part):
        for pair in range(2):
            xn = normed[pl.ds(2 * pair, 2)].reshape(2 * CAP, dim)
            hidden[pl.ds(2 * pair, 2), :, pl.ds(part * width, width)] = activate(xn, part).reshape(2, CAP, width)

    own_rows(0)
    weights[0].wait_recv()
    weights[1].wait_recv()
    own_rows(1)
    weights[2].wait_recv()

    def partial(src):
        return pltpu.make_async_remote_copy(
            mate_part.at[src], got_part.at[src], part_s.at[src], part_r.at[src],
            device_id=tmate, device_id_type=MESH)

    def giveback(src):
        return pltpu.make_async_remote_copy(
            summed.at[src], back.at[y], ret_s.at[src], ret_r.at[y],
            device_id=at_row(src), device_id_type=MESH)

    tile = dim // 4

    @pl.loop(0, 5)
    def _(b):
        @pl.when(b < 4)
        def _():
            src = block(b)
            relay(src).wait_recv()
            xn = norm(1, src)
            hid = jnp.concatenate([activate(xn, 0), activate(xn, 1)], axis=1)
            for t in range(4):
                cols = pl.ds(t * tile, tile)
                mate_part[src, :, cols] = jnp.dot(hid, wd[:, cols], preferred_element_type=F32).astype(BF16)
            partial(src).start()

            @pl.when(b + EARLY < 4)
            def _():
                relay(block(b + EARLY)).start()

            hid = hidden[src]
            for t in range(4):
                cols = pl.ds(t * tile, tile)
                own_part[src, :, cols] = jnp.dot(hid, wd[:, cols], preferred_element_type=F32)

        @pl.when(b > 0)
        def _():
            src = block(b - 1)
            partial(src).wait_recv()
            total = (own_part[src] + got_part[src].astype(F32)).astype(BF16)

            @pl.when(b < 4)
            def _():
                summed[src] = total
                giveback(src).start()

            @pl.when(b == 4)
            def _():
                back[y] = total

    for i in range(1, 4):
        g = lax.rem(y + i, 4)
        pltpu.make_async_remote_copy(
            summed.at[0], back.at[g], ret_s.at[0], ret_r.at[g],
            device_id=at_row(g), device_id_type=MESH).wait_recv()

    for t in range(4):
        cols = pl.ds(t * tile, tile)
        total = inc[:, cols].astype(F32)
        for g in range(NEXP):
            total = total + gate_of[:, g:g + 1] * jnp.dot(
                place_t[g][:, :CAP], back[g, :, cols], preferred_element_type=F32)
        out[:, cols] = total.astype(BF16)

    for i in range(SHIFT_PARTS):
        shift(i, nxt).wait_send()

    @pl.when(enters)
    def _():
        for i in range(SHIFT_PARTS):
            second_leg(i).wait_send()

    for copy in weights:
        copy.wait_send()
    for k in range(3):
        dispatch(k).wait_send()
    for i in range(4):
        relay(i).wait_send()
        partial(i).wait_send()
    for i in range(1, 4):
        giveback(lax.rem(y + i, 4)).wait_send()


def local(acts, routes, gates, norm_gain, gate_w, up_w, down_w):
    tok, dim = acts.shape[1:]
    width = gate_w.shape[2]
    hbm = pl.BlockSpec(memory_space=pl.ANY)
    vmem = pl.BlockSpec(memory_space=pltpu.VMEM)
    dma = pltpu.SemaphoreType.DMA
    result = pl.pallas_call(
        kernel,
        name="relay_experts",
        out_shape=jax.ShapeDtypeStruct((tok, dim), BF16),
        in_specs=[hbm, vmem, vmem, vmem, hbm, hbm, hbm],
        out_specs=vmem,
        scratch_shapes=[
            pltpu.VMEM((tok, dim), BF16),
            pltpu.VMEM((tok, dim), BF16),
            pltpu.VMEM((3, CAP, dim), BF16),
            pltpu.VMEM((2, 4, CAP, dim), BF16),
            pltpu.VMEM((2, dim, width), BF16),
            pltpu.VMEM((2, dim, width), BF16),
            pltpu.VMEM((2 * width, dim), BF16),
            pltpu.VMEM((4, CAP, dim), BF16),
            pltpu.VMEM((4, CAP, 2 * width), BF16),
            pltpu.VMEM((4, CAP, dim), F32),
            pltpu.VMEM((4, CAP, dim), BF16),
            pltpu.VMEM((4, CAP, dim), BF16),
            pltpu.VMEM((4, CAP, dim), BF16),
            pltpu.VMEM((4, CAP, dim), BF16),
            pltpu.VMEM((4, tok, tok), BF16),
            pltpu.VMEM((4, tok, tok), BF16),
            pltpu.VMEM((tok, tok), F32),
            dma((SHIFT_PARTS,)), dma((SHIFT_PARTS,)),
            dma((SHIFT_PARTS,)), dma((SHIFT_PARTS,)),
            dma((3,)), dma((3,)), dma((3,)),
            dma((3,)), dma((4,)),
            dma((4,)), dma((4,)),
            dma((4,)), dma((4,)),
            dma((4,)), dma((4,)),
        ],
        compiler_params=pltpu.CompilerParams(
            collective_id=0, has_side_effects=True, vmem_limit_bytes=56 * 1024 * 1024),
    )(acts[0], routes[0].T, gates[0].T, norm_gain, gate_w[0], up_w[0], down_w[0])
    return result.reshape(1, tok, dim)


def solution(mesh):
    in_specs = (
        P("section", "expert", None),
        P("section", "expert", None),
        P("section", "expert", None),
        P("section", None),
        P("section", None, "expert"),
        P("section", None, "expert"),
        P("section", "expert", None),
    )
    out_specs = P("section", "expert", None)
    return jax.shard_map(local, mesh=mesh, in_specs=in_specs, out_specs=out_specs, check_vma=False)
```

```python
import functools

import jax
import jax.numpy as jnp
from jax import lax
from jax.experimental import pallas as pl
from jax.experimental.pallas import tpu as pltpu
from jax.sharding import PartitionSpec as P

NEXP = 4
CAP = 96
SHIFT_PARTS = 4
EARLY = 1
SOON = 2
PARTS = 2
PAIR = 1
LAG = 2
JOIN = 1
MESH = pl.DeviceIdType.MESH
F32 = jnp.float32
BF16 = jnp.bfloat16


def far_order(y, k):
    low = y < 2
    yy = jnp.where(low, y, 3 - y)
    d = 3 - k
    d = jnp.where(d <= yy, d - 1, d)
    return jnp.where(low, d, 3 - d)


def kernel(
    acts, routes, gates, gain, gate_w, up_w, down_w, out,
    inc, hop, packs, far_rows, onward, rows, wg, wu, wd, normed, mate_normed, hidden, mate_hidden, own_part, mate_part, got_part,
    summed, back, via, joined, given_in, total, place_t, place, gate_of, far_routes, far_gates, far_place, far_pick, far_gate_of,
    shift_s, shift_r, hop_s, hop_r, w_s, w_r, w_l, y_s, y_r, rel_s, rel_r, part_s, part_r, ret_s, ret_r,
    via_r, join_s, join_r, meta_s, meta_r, far_s, far_r, on_s,
):
    tok, dim = inc.shape
    width = gate_w.shape[1]
    n_sec = lax.axis_size("section")
    half = n_sec // 2
    s = lax.axis_index("section")
    e = lax.axis_index("expert")
    core = lax.rem(s, 2)
    x = lax.rem(e, 4)
    y = e // 4
    flip = x + 1 - 2 * lax.rem(x, 2)
    cross = 3 - x
    wx = jnp.where(core == 0, flip, cross)
    tx = jnp.where(core == 0, cross, flip)
    nxt = (lax.rem(s + 1, n_sec), e)
    prv = (lax.rem(s + n_sec - 1, n_sec), e)
    wmate = (s, y * 4 + wx)
    tmate = (s, y * 4 + tx)
    leaves = lax.rem(s, half) == half - 1
    enters = lax.rem(s, half) == 0
    ring = (s // half) * 4 + y

    def around(steps, last):
        to = lax.rem(ring + 8 + steps, 8)
        return ((to // 4) * half + last * (half - 1), lax.rem(to, 4) * 4 + x)

    def at_row(r):
        return (s, r * 4 + x)

    def greet(peer):
        pl.semaphore_signal(barrier, inc=1, device_id=peer, device_id_type=MESH)

    barrier = pltpu.get_barrier_semaphore()
    greet(wmate)
    greet(tmate)
    for i in range(1, 4):
        greet(at_row(lax.rem(y + i, 4)))

    @pl.when(enters)
    def _():
        for last in range(2):
            greet(around(2, last))
            greet(around(-2, last))

    @pl.when(jnp.logical_not(enters))
    def _():
        greet(prv)

    local = [
        pltpu.make_async_copy(gate_w, wg.at[0], w_l.at[0]),
        pltpu.make_async_copy(up_w, wu.at[0], w_l.at[1]),
        pltpu.make_async_copy(down_w, wd.at[pl.ds(0, width)], w_l.at[2]),
    ]
    for copy in local:
        copy.start()
    pl.semaphore_wait(barrier, 6 + jnp.where(leaves, 1, 0) + jnp.where(enters, 2, 0))

    part = dim // SHIFT_PARTS
    columns = [pl.ds(i * part, part) for i in range(SHIFT_PARTS)]

    def shift(i, peer):
        return pltpu.make_async_remote_copy(
            acts.at[:, columns[i]], inc.at[:, columns[i]],
            shift_s.at[i], shift_r.at[i], device_id=peer, device_id_type=MESH)

    def first_leg(i):
        return pltpu.make_async_remote_copy(
            acts.at[:, columns[i]], hop.at[:, columns[i]], shift_s.at[i], hop_r.at[i],
            device_id=around(2 if i % 2 == 0 else -2, 0), device_id_type=MESH)

    def second_leg(i):
        return pltpu.make_async_remote_copy(
            hop.at[:, columns[i]], inc.at[:, columns[i]], hop_s.at[i], shift_r.at[i],
            device_id=around(2 if i % 2 == 0 else -2, 0), device_id_type=MESH)

    @pl.when(leaves)
    def _():
        for i in range(SHIFT_PARTS):
            first_leg(i).start()

    @pl.when(jnp.logical_not(leaves))
    def _():
        for i in range(SHIFT_PARTS):
            shift(i, nxt).start()

    tile = dim // PARTS
    narrow = [
        pltpu.make_async_remote_copy(src, dst.at[1], w_s.at[i], w_r.at[i], device_id=wmate, device_id_type=MESH)
        for i, (src, dst) in enumerate(((gate_w, wg), (up_w, wu)))
    ]

    def columns_of(h):
        return pl.ds(pl.multiple_of(h * tile, tile), tile)

    def wide(h):
        return pltpu.make_async_remote_copy(
            down_w.at[:, columns_of(h)], wd.at[pl.ds(width, width), columns_of(h)], w_s.at[2 + h], w_r.at[2 + h],
            device_id=wmate, device_id_type=MESH)

    for copy in narrow:
        copy.start()
    for h in range(PARTS):
        wide(h).start()

    inner = (y == 1) | (y == 2)
    mate = y + 1 - 2 * lax.rem(y, 2)
    across = jnp.where(y < 2, 2, 1)
    mine = jnp.where(inner, 1, 0)
    meta = [
        pltpu.make_async_remote_copy(
            src, dst.at[mine], meta_s.at[i], meta_r.at[mine, i], device_id=at_row(across), device_id_type=MESH)
        for i, (src, dst) in enumerate(((routes, far_routes), (gates, far_gates)))
    ]
    for copy in meta:
        copy.start()

    lane = lax.broadcasted_iota(jnp.int32, (tok, tok), 1)
    sub = lax.broadcasted_iota(jnp.int32, (tok, tok), 0)
    slot = sub.astype(F32)

    def table(ids, weights):
        first, second = ids[0:1, :] == sub, ids[1:2, :] == sub
        member = (first | second).astype(F32)
        gate = jnp.where(first, weights[0:1, :], 0.0) + jnp.where(second, weights[1:2, :], 0.0)
        rank = jnp.dot(member.astype(BF16), (sub <= lane).astype(BF16), preferred_element_type=F32) - 1.0
        hots = [jnp.where(rank[g:g + 1, :] == slot, member[g:g + 1, :], 0.0) for g in range(NEXP)]
        return gate.T, hots

    gate_of[...], hots = table(routes[...], gates[...])
    for g in range(NEXP):
        place[g] = hots[g].astype(BF16)
        place_t[g] = hots[g].T.astype(BF16)

    @pl.when(enters)
    def _():
        for i in range(SHIFT_PARTS):
            first_leg(i).wait_recv()
            second_leg(i).start()

    def packed(g, cols):
        return jnp.dot(place[g][:CAP], inc[:, cols], preferred_element_type=F32).astype(BF16)

    def crossing(i, to):
        return pltpu.make_async_remote_copy(
            inc.at[:, columns[i]], far_rows.at[to, :, columns[i]], far_s.at[i], far_r.at[to, i],
            device_id=at_row(across), device_id_type=MESH)

    for i in range(SHIFT_PARTS):
        shift(i, nxt).wait_recv()
        cols = columns[i]
        crossing(i, mine).start()
        packs[:, cols] = packed(mate, cols)
        rows[0, y, :, cols] = packed(y, cols)

    dispatch = pltpu.make_async_remote_copy(
        packs, rows.at[0, y], y_s.at[0], y_r.at[y], device_id=at_row(mate), device_id_type=MESH)
    dispatch.start()

    def passing(b, i):
        src = far_order(y, b)
        return pltpu.make_async_remote_copy(
            onward.at[b, :, columns[i]], rows.at[0, src, :, columns[i]], on_s.at[b, i], y_r.at[src],
            device_id=at_row(mate), device_id_type=MESH)

    @pl.when(inner)
    def _():
        for i in range(2):
            for j, (src, dst) in enumerate(((routes, far_routes), (gates, far_gates))):
                pltpu.make_async_remote_copy(
                    src, dst.at[i], meta_s.at[j], meta_r.at[i, j], device_id=at_row(across),
                    device_id_type=MESH).wait_recv()
            far_gate_of[i], far_hots = table(far_routes[i], far_gates[i])
            for g in range(NEXP):
                far_pick[i, g] = far_hots[g].astype(BF16)
                far_place[i, g] = far_hots[g].T.astype(BF16)
        for i in range(SHIFT_PARTS):
            for b in range(2):
                crossing(i, b).wait_recv()
                value = far_rows[b, :, columns[i]]
                onward[b, :, columns[i]] = jnp.dot(
                    far_pick[b, mate][:CAP], value, preferred_element_type=F32).astype(BF16)
                passing(b, i).start()
                rows[0, far_order(y, b), :, columns[i]] = jnp.dot(
                    far_pick[b, y][:CAP], value, preferred_element_type=F32).astype(BF16)

    def arrival(src):
        return pltpu.make_async_remote_copy(
            packs, rows.at[0, src], y_s.at[0], y_r.at[src],
            device_id=at_row(mate), device_id_type=MESH)

    def relay(src):
        return pltpu.make_async_remote_copy(
            rows.at[0, src], rows.at[1, src], rel_s.at[src], rel_r.at[src],
            device_id=tmate, device_id_type=MESH)

    def block(b):
        return jnp.where(b == 3, y, far_order(y, jnp.minimum(b, 2)))

    def norm(which, src):
        xf = rows[which, src].astype(F32)
        scale = lax.rsqrt(jnp.mean(xf * xf, axis=1, keepdims=True) + 1e-06)
        return (xf * scale * gain[...]).astype(BF16)

    def activate(xn, part):
        gpart = jnp.dot(xn, wg[part], preferred_element_type=F32)
        upart = jnp.dot(xn, wu[part], preferred_element_type=F32)
        return (jax.nn.silu(gpart) * upart).astype(BF16)

    @pl.when(enters)
    def _():
        relay(y).start()

    normed[y] = norm(0, y)

    @pl.loop(0, 3)
    def _(b):
        src = block(b)

        @pl.when((b == 2) | jnp.logical_not(inner))
        def _():
            arrival(src).wait_recv()

        @pl.when((b < EARLY) | enters)
        def _():
            relay(src).start()

        normed[src] = norm(0, src)

    for copy in local:
        copy.wait()

    def own_rows(part):
        for pair in range(2):
            xn = normed[pl.ds(2 * pair, 2)].reshape(2 * CAP, dim)
            hidden[pl.ds(2 * pair, 2), :, pl.ds(part * width, width)] = activate(xn, part).reshape(2, CAP, width)

    own_rows(0)
    relay(block(0)).wait_recv()
    mate_normed[...] = norm(1, block(0))
    mate_hidden[block(0), :, pl.ds(0, width)] = activate(mate_normed[...], 0)
    narrow[0].wait_recv()

    @pl.when(jnp.logical_not(enters))
    def _():
        for b in range(EARLY, SOON):
            relay(block(b)).start()

    narrow[1].wait_recv()

    def partial(src, h):
        return pltpu.make_async_remote_copy(
            mate_part.at[src, :, columns_of(h)], got_part.at[src, :, columns_of(h)], part_s.at[src, h], part_r.at[src, h],
            device_id=tmate, device_id_type=MESH)

    def giveback(src, h):
        return pltpu.make_async_remote_copy(
            summed.at[src, :, columns_of(h)], back.at[y, :, columns_of(h)], ret_s.at[src, h], ret_r.at[h],
            device_id=at_row(mate), device_id_type=MESH)

    def inward(b, h):
        return pltpu.make_async_remote_copy(
            summed.at[block(b), :, columns_of(h)], via.at[b, :, columns_of(h)], ret_s.at[block(b), h], via_r.at[b, h],
            device_id=at_row(mate), device_id_type=MESH)

    def outward(b, h):
        return pltpu.make_async_remote_copy(
            joined.at[b, :, columns_of(h)], given_in.at[:, columns_of(h)], join_s.at[b, h], join_r.at[h],
            device_id=at_row(block(b)), device_id_type=MESH)

    def lift(gate, hot, value, g):
        gate = jnp.sum(jnp.where(lane == g, gate, 0.0), axis=1, keepdims=True)
        return gate * jnp.dot(hot[:, :CAP], value, preferred_element_type=F32)

    def item(i):
        i = jnp.maximum(i, 0)
        j = lax.rem(i, PAIR * PARTS)
        return i // (PAIR * PARTS) * PAIR + lax.rem(j, PAIR), j // PAIR

    @pl.loop(0, 4 * PARTS + LAG + JOIN)
    def _(i):
        @pl.when(i < 4 * PARTS)
        def _():
            b, h = item(i)
            src = block(b)
            cols = columns_of(h)

            @pl.when((h == 0) & (b > 0))
            def _():
                relay(src).wait_recv()
                mate_normed[...] = norm(1, src)
                mate_hidden[src, :, pl.ds(0, width)] = activate(mate_normed[...], 0)

            @pl.when(h == 0)
            def _():
                mate_hidden[src, :, pl.ds(width, width)] = activate(mate_normed[...], 1)

            @pl.when(b == 0)
            def _():
                wide(h).wait_recv()

            mate_part[src, :, cols] = jnp.dot(
                mate_hidden[src], wd[:, cols], preferred_element_type=F32).astype(BF16)
            partial(src, h).start()

            @pl.when((h == 0) & (b + SOON < 4) & jnp.logical_not(enters))
            def _():
                relay(block(b + SOON)).start()

            @pl.when(i == 0)
            def _():
                own_rows(1)

            own_part[src, :, cols] = jnp.dot(hidden[src], wd[:, cols], preferred_element_type=F32)

        @pl.when((i >= LAG) & (i < 4 * PARTS + LAG))
        def _():
            b, h = item(i - LAG)
            src = block(b)
            cols = columns_of(h)
            partial(src, h).wait_recv()
            value = (own_part[src, :, cols] + got_part[src, :, cols].astype(F32)).astype(BF16)

            @pl.when(b < 3)
            def _():
                summed[src, :, cols] = value

            @pl.when((b < 2) & jnp.logical_not(inner))
            def _():
                inward(b, h).start()

            @pl.when(b == 2)
            def _():
                giveback(src, h).start()

            @pl.when(b == 3)
            def _():
                back[y, :, cols] = value

        @pl.when(inner & (i >= LAG + JOIN))
        def _():
            b, h = item(i - LAG - JOIN)

            @pl.when(b < 2)
            def _():
                cols = columns_of(h)
                inward(b, h).wait_recv()
                gate = far_gate_of[b]
                joined[b, :, cols] = (
                    lift(gate, far_place[b, y], summed[block(b), :, cols], y)
                    + lift(gate, far_place[b, mate], via[b, :, cols], mate)).astype(BF16)
                outward(b, h).start()

    for h in range(PARTS):
        cols = pl.ds(h * tile, tile)
        total[:, cols] = inc[:, cols].astype(F32) + lift(gate_of[...], place_t[y], back[y, :, cols], y)

    for h in range(PARTS):
        cols = pl.ds(h * tile, tile)
        pltpu.make_async_remote_copy(
            summed.at[0, :, cols], back.at[mate, :, cols], ret_s.at[0, h], ret_r.at[h],
            device_id=at_row(mate), device_id_type=MESH).wait_recv()
        total[:, cols] = total[:, cols] + lift(gate_of[...], place_t[mate], back[mate, :, cols], mate)

    for h in range(PARTS):
        cols = pl.ds(h * tile, tile)
        outward(0, h).wait_recv()
        out[:, cols] = (total[:, cols] + given_in[:, cols].astype(F32)).astype(out.dtype)

    for copy in meta:
        copy.wait_send()

    for i in range(SHIFT_PARTS):
        shift(i, nxt).wait_send()

    @pl.when(enters)
    def _():
        for i in range(SHIFT_PARTS):
            second_leg(i).wait_send()

    for copy in narrow:
        copy.wait_send()
    for h in range(PARTS):
        wide(h).wait_send()
    dispatch.wait_send()
    for i in range(SHIFT_PARTS):
        crossing(i, mine).wait_send()

    @pl.when(inner)
    def _():
        for b in range(2):
            for i in range(SHIFT_PARTS):
                passing(b, i).wait_send()

    for i in range(4):
        relay(i).wait_send()
        for h in range(PARTS):
            partial(i, h).wait_send()
    for h in range(PARTS):
        giveback(mate, h).wait_send()
        for b in range(2):
            @pl.when(inner)
            def _():
                outward(b, h).wait_send()

            @pl.when(jnp.logical_not(inner))
            def _():
                inward(b, h).wait_send()


def local(acts, routes, gates, norm_gain, gate_w, up_w, down_w):
    tok, dim = acts.shape[1:]
    width = gate_w.shape[2]
    hbm = pl.BlockSpec(memory_space=pl.ANY)
    vmem = pl.BlockSpec(memory_space=pltpu.VMEM)
    dma = pltpu.SemaphoreType.DMA
    result = pl.pallas_call(
        kernel,
        name="relay_experts",
        out_shape=jax.ShapeDtypeStruct((tok, dim), BF16),
        in_specs=[hbm, vmem, vmem, vmem, hbm, hbm, hbm],
        out_specs=vmem,
        scratch_shapes=[
            pltpu.VMEM((tok, dim), BF16),
            pltpu.VMEM((tok, dim), BF16),
            pltpu.VMEM((CAP, dim), BF16),
            pltpu.VMEM((2, tok, dim), BF16),
            pltpu.VMEM((2, CAP, dim), BF16),
            pltpu.VMEM((2, 4, CAP, dim), BF16),
            pltpu.VMEM((2, dim, width), BF16),
            pltpu.VMEM((2, dim, width), BF16),
            pltpu.VMEM((2 * width, dim), BF16),
            pltpu.VMEM((4, CAP, dim), BF16),
            pltpu.VMEM((CAP, dim), BF16),
            pltpu.VMEM((4, CAP, 2 * width), BF16),
            pltpu.VMEM((4, CAP, 2 * width), BF16),
            pltpu.VMEM((4, CAP, dim), F32),
            pltpu.VMEM((4, CAP, dim), BF16),
            pltpu.VMEM((4, CAP, dim), BF16),
            pltpu.VMEM((4, CAP, dim), BF16),
            pltpu.VMEM((4, CAP, dim), BF16),
            pltpu.VMEM((2, CAP, dim), BF16),
            pltpu.VMEM((2, tok, dim), BF16),
            pltpu.VMEM((tok, dim), BF16),
            pltpu.VMEM((tok, dim), F32),
            pltpu.VMEM((4, tok, tok), BF16),
            pltpu.VMEM((4, tok, tok), BF16),
            pltpu.VMEM((tok, tok), F32),
            pltpu.VMEM((2, 2, tok), jnp.int32),
            pltpu.VMEM((2, 2, tok), F32),
            pltpu.VMEM((2, 4, tok, tok), BF16),
            pltpu.VMEM((2, 4, tok, tok), BF16),
            pltpu.VMEM((2, tok, tok), F32),
            dma((SHIFT_PARTS,)), dma((SHIFT_PARTS,)),
            dma((SHIFT_PARTS,)), dma((SHIFT_PARTS,)),
            dma((2 + PARTS,)), dma((2 + PARTS,)), dma((3,)),
            dma((1,)), dma((4,)),
            dma((4,)), dma((4,)),
            dma((4, PARTS)), dma((4, PARTS)),
            dma((4, PARTS)), dma((PARTS,)),
            dma((2, PARTS)), dma((2, PARTS)), dma((PARTS,)), dma((2,)), dma((2, 2)),
            dma((SHIFT_PARTS,)), dma((2, SHIFT_PARTS)), dma((2, SHIFT_PARTS)),
        ],
        compiler_params=pltpu.CompilerParams(
            collective_id=0, has_side_effects=True, vmem_limit_bytes=56 * 1024 * 1024),
    )(acts[0], routes[0].T, gates[0].T, norm_gain, gate_w[0], up_w[0], down_w[0])
    return result.reshape(1, tok, dim)


def solution(mesh):
    in_specs = (
        P("section", "expert", None),
        P("section", "expert", None),
        P("section", "expert", None),
        P("section", None),
        P("section", None, "expert"),
        P("section", None, "expert"),
        P("section", "expert", None),
    )
    out_specs = P("section", "expert", None)
    return jax.shard_map(local, mesh=mesh, in_specs=in_specs, out_specs=out_specs, check_vma=False)
```

```python
import functools

import jax
import jax.numpy as jnp
from jax import lax
from jax.experimental import pallas as pl
from jax.experimental.pallas import tpu as pltpu
from jax.sharding import PartitionSpec as P

NEXP = 4
CAP = 96
SHIFT_PARTS = 4
EARLY = 1
SOON = 2
PARTS = 2
PAIR = 1
LAG = 2
JOIN = 2
MESH = pl.DeviceIdType.MESH
F32 = jnp.float32
BF16 = jnp.bfloat16


def far_order(y, k):
    low = y < 2
    yy = jnp.where(low, y, 3 - y)
    d = 3 - k
    d = jnp.where(d <= yy, d - 1, d)
    return jnp.where(low, d, 3 - d)


def kernel(
    acts, routes, gates, gain, gate_w, up_w, down_w, out,
    inc, hop, packs, rows, wg, wu, wd, normed, mate_normed, hidden, mate_hidden, own_part, mate_part, got_part,
    summed, back, via, joined, given_in, total, place_t, place, gate_of, far_routes, far_gates, far_place, far_gate_of,
    shift_s, shift_r, hop_s, hop_r, w_s, w_r, w_l, y_s, y_r, rel_s, rel_r, part_s, part_r, ret_s, ret_r,
    via_r, join_s, join_r, meta_s, meta_r,
):
    tok, dim = inc.shape
    width = gate_w.shape[1]
    n_sec = lax.axis_size("section")
    half = n_sec // 2
    s = lax.axis_index("section")
    e = lax.axis_index("expert")
    core = lax.rem(s, 2)
    x = lax.rem(e, 4)
    y = e // 4
    flip = x + 1 - 2 * lax.rem(x, 2)
    cross = 3 - x
    wx = jnp.where(core == 0, flip, cross)
    tx = jnp.where(core == 0, cross, flip)
    nxt = (lax.rem(s + 1, n_sec), e)
    prv = (lax.rem(s + n_sec - 1, n_sec), e)
    wmate = (s, y * 4 + wx)
    tmate = (s, y * 4 + tx)
    leaves = lax.rem(s, half) == half - 1
    enters = lax.rem(s, half) == 0
    ring = (s // half) * 4 + y

    def around(steps, last):
        to = lax.rem(ring + 8 + steps, 8)
        return ((to // 4) * half + last * (half - 1), lax.rem(to, 4) * 4 + x)

    def at_row(r):
        return (s, r * 4 + x)

    def greet(peer):
        pl.semaphore_signal(barrier, inc=1, device_id=peer, device_id_type=MESH)

    barrier = pltpu.get_barrier_semaphore()
    greet(wmate)
    greet(tmate)
    for i in range(1, 4):
        greet(at_row(lax.rem(y + i, 4)))

    @pl.when(enters)
    def _():
        for last in range(2):
            greet(around(2, last))
            greet(around(-2, last))

    @pl.when(jnp.logical_not(enters))
    def _():
        greet(prv)

    local = [
        pltpu.make_async_copy(gate_w, wg.at[0], w_l.at[0]),
        pltpu.make_async_copy(up_w, wu.at[0], w_l.at[1]),
        pltpu.make_async_copy(down_w, wd.at[pl.ds(0, width)], w_l.at[2]),
    ]
    for copy in local:
        copy.start()
    pl.semaphore_wait(barrier, 6 + jnp.where(leaves, 1, 0) + jnp.where(enters, 2, 0))

    part = dim // SHIFT_PARTS
    columns = [pl.ds(i * part, part) for i in range(SHIFT_PARTS)]

    def shift(i, peer):
        return pltpu.make_async_remote_copy(
            acts.at[:, columns[i]], inc.at[:, columns[i]],
            shift_s.at[i], shift_r.at[i], device_id=peer, device_id_type=MESH)

    def first_leg(i):
        return pltpu.make_async_remote_copy(
            acts.at[:, columns[i]], hop.at[:, columns[i]], shift_s.at[i], hop_r.at[i],
            device_id=around(2 if i % 2 == 0 else -2, 0), device_id_type=MESH)

    def second_leg(i):
        return pltpu.make_async_remote_copy(
            hop.at[:, columns[i]], inc.at[:, columns[i]], hop_s.at[i], shift_r.at[i],
            device_id=around(2 if i % 2 == 0 else -2, 0), device_id_type=MESH)

    @pl.when(leaves)
    def _():
        for i in range(SHIFT_PARTS):
            first_leg(i).start()

    @pl.when(jnp.logical_not(leaves))
    def _():
        for i in range(SHIFT_PARTS):
            shift(i, nxt).start()

    tile = dim // PARTS
    narrow = [
        pltpu.make_async_remote_copy(src, dst.at[1], w_s.at[i], w_r.at[i], device_id=wmate, device_id_type=MESH)
        for i, (src, dst) in enumerate(((gate_w, wg), (up_w, wu)))
    ]

    def columns_of(h):
        return pl.ds(pl.multiple_of(h * tile, tile), tile)

    def wide(h):
        return pltpu.make_async_remote_copy(
            down_w.at[:, columns_of(h)], wd.at[pl.ds(width, width), columns_of(h)], w_s.at[2 + h], w_r.at[2 + h],
            device_id=wmate, device_id_type=MESH)

    for copy in narrow:
        copy.start()
    for h in range(PARTS):
        wide(h).start()

    inner = (y == 1) | (y == 2)
    mate = y + 1 - 2 * lax.rem(y, 2)
    across = jnp.where(y < 2, 2, 1)
    mine = jnp.where(inner, 1, 0)
    meta = [
        pltpu.make_async_remote_copy(
            src, dst.at[mine], meta_s.at[i], meta_r.at[mine, i], device_id=at_row(across), device_id_type=MESH)
        for i, (src, dst) in enumerate(((routes, far_routes), (gates, far_gates)))
    ]
    for copy in meta:
        copy.start()

    lane = lax.broadcasted_iota(jnp.int32, (tok, tok), 1)
    sub = lax.broadcasted_iota(jnp.int32, (tok, tok), 0)
    slot = sub.astype(F32)

    def table(ids, weights):
        first, second = ids[0:1, :] == sub, ids[1:2, :] == sub
        member = (first | second).astype(F32)
        gate = jnp.where(first, weights[0:1, :], 0.0) + jnp.where(second, weights[1:2, :], 0.0)
        rank = jnp.dot(member.astype(BF16), (sub <= lane).astype(BF16), preferred_element_type=F32) - 1.0
        hots = [jnp.where(rank[g:g + 1, :] == slot, member[g:g + 1, :], 0.0) for g in range(NEXP)]
        return gate.T, hots

    gate_of[...], hots = table(routes[...], gates[...])
    for g in range(NEXP):
        place[g] = hots[g].astype(BF16)
        place_t[g] = hots[g].T.astype(BF16)

    @pl.when(enters)
    def _():
        for i in range(SHIFT_PARTS):
            first_leg(i).wait_recv()
            second_leg(i).start()

    def packed(g, cols):
        return jnp.dot(place[g][:CAP], inc[:, cols], preferred_element_type=F32).astype(BF16)

    for i in range(SHIFT_PARTS):
        shift(i, nxt).wait_recv()
        cols = columns[i]
        for k in range(3):
            packs[k, :, cols] = packed(far_order(y, k), cols)
        rows[0, y, :, cols] = packed(y, cols)

    def dispatch(k):
        return pltpu.make_async_remote_copy(
            packs.at[k], rows.at[0, y], y_s.at[k], y_r.at[y],
            device_id=at_row(far_order(y, k)), device_id_type=MESH)

    for k in range(3):
        dispatch(k).start()

    @pl.when(inner)
    def _():
        for i in range(2):
            for j, (src, dst) in enumerate(((routes, far_routes), (gates, far_gates))):
                pltpu.make_async_remote_copy(
                    src, dst.at[i], meta_s.at[j], meta_r.at[i, j], device_id=at_row(across),
                    device_id_type=MESH).wait_recv()
            far_gate_of[i], far_hots = table(far_routes[i], far_gates[i])
            for g in range(NEXP):
                far_place[i, g] = far_hots[g].T.astype(BF16)

    def arrival(src):
        return pltpu.make_async_remote_copy(
            packs.at[0], rows.at[0, src], y_s.at[0], y_r.at[src],
            device_id=at_row(src), device_id_type=MESH)

    def relay(src):
        return pltpu.make_async_remote_copy(
            rows.at[0, src], rows.at[1, src], rel_s.at[src], rel_r.at[src],
            device_id=tmate, device_id_type=MESH)

    def block(b):
        return jnp.where(b == 3, y, far_order(y, jnp.minimum(b, 2)))

    def norm(which, src):
        xf = rows[which, src].astype(F32)
        scale = lax.rsqrt(jnp.mean(xf * xf, axis=1, keepdims=True) + 1e-06)
        return (xf * scale * gain[...]).astype(BF16)

    def activate(xn, part):
        gpart = jnp.dot(xn, wg[part], preferred_element_type=F32)
        upart = jnp.dot(xn, wu[part], preferred_element_type=F32)
        return (jax.nn.silu(gpart) * upart).astype(BF16)

    @pl.when(enters)
    def _():
        relay(y).start()

    normed[y] = norm(0, y)

    @pl.loop(0, 3)
    def _(b):
        src = block(b)
        arrival(src).wait_recv()

        @pl.when((b < EARLY) | enters)
        def _():
            relay(src).start()

        normed[src] = norm(0, src)

    for copy in local:
        copy.wait()

    def own_rows(part):
        for pair in range(2):
            xn = normed[pl.ds(2 * pair, 2)].reshape(2 * CAP, dim)
            hidden[pl.ds(2 * pair, 2), :, pl.ds(part * width, width)] = activate(xn, part).reshape(2, CAP, width)

    own_rows(0)
    relay(block(0)).wait_recv()
    mate_normed[...] = norm(1, block(0))
    mate_hidden[block(0), :, pl.ds(0, width)] = activate(mate_normed[...], 0)
    narrow[0].wait_recv()

    @pl.when(jnp.logical_not(enters))
    def _():
        for b in range(EARLY, SOON):
            relay(block(b)).start()

    narrow[1].wait_recv()

    def partial(src, h):
        return pltpu.make_async_remote_copy(
            mate_part.at[src, :, columns_of(h)], got_part.at[src, :, columns_of(h)], part_s.at[src, h], part_r.at[src, h],
            device_id=tmate, device_id_type=MESH)

    def giveback(src, h):
        return pltpu.make_async_remote_copy(
            summed.at[src, :, columns_of(h)], back.at[y, :, columns_of(h)], ret_s.at[src, h], ret_r.at[h],
            device_id=at_row(mate), device_id_type=MESH)

    def inward(b, h):
        return pltpu.make_async_remote_copy(
            summed.at[block(b), :, columns_of(h)], via.at[b, :, columns_of(h)], ret_s.at[block(b), h], via_r.at[b, h],
            device_id=at_row(mate), device_id_type=MESH)

    def outward(b, h):
        return pltpu.make_async_remote_copy(
            joined.at[b, :, columns_of(h)], given_in.at[:, columns_of(h)], join_s.at[b, h], join_r.at[h],
            device_id=at_row(block(b)), device_id_type=MESH)

    def lift(gate, hot, value, g):
        gate = jnp.sum(jnp.where(lane == g, gate, 0.0), axis=1, keepdims=True)
        return gate * jnp.dot(hot[:, :CAP], value, preferred_element_type=F32)

    def item(i):
        i = jnp.maximum(i, 0)
        j = lax.rem(i, PAIR * PARTS)
        return i // (PAIR * PARTS) * PAIR + lax.rem(j, PAIR), j // PAIR

    @pl.loop(0, 4 * PARTS + LAG + JOIN)
    def _(i):
        @pl.when(i < 4 * PARTS)
        def _():
            b, h = item(i)
            src = block(b)
            cols = columns_of(h)

            @pl.when((h == 0) & (b > 0))
            def _():
                relay(src).wait_recv()
                mate_normed[...] = norm(1, src)
                mate_hidden[src, :, pl.ds(0, width)] = activate(mate_normed[...], 0)

            @pl.when(h == 0)
            def _():
                mate_hidden[src, :, pl.ds(width, width)] = activate(mate_normed[...], 1)

            @pl.when(b == 0)
            def _():
                wide(h).wait_recv()

            mate_part[src, :, cols] = jnp.dot(
                mate_hidden[src], wd[:, cols], preferred_element_type=F32).astype(BF16)
            partial(src, h).start()

            @pl.when((h == 0) & (b + SOON < 4) & jnp.logical_not(enters))
            def _():
                relay(block(b + SOON)).start()

            @pl.when(i == 0)
            def _():
                own_rows(1)

            own_part[src, :, cols] = jnp.dot(hidden[src], wd[:, cols], preferred_element_type=F32)

        @pl.when((i >= LAG) & (i < 4 * PARTS + LAG))
        def _():
            b, h = item(i - LAG)
            src = block(b)
            cols = columns_of(h)
            partial(src, h).wait_recv()
            value = (own_part[src, :, cols] + got_part[src, :, cols].astype(F32)).astype(BF16)

            @pl.when(b < 3)
            def _():
                summed[src, :, cols] = value

            @pl.when((b < 2) & jnp.logical_not(inner))
            def _():
                inward(b, h).start()

            @pl.when(b == 2)
            def _():
                giveback(src, h).start()

            @pl.when(b == 3)
            def _():
                back[y, :, cols] = value

        @pl.when(inner & (i >= LAG + JOIN))
        def _():
            b, h = item(i - LAG - JOIN)

            @pl.when(b < 2)
            def _():
                cols = columns_of(h)
                inward(b, h).wait_recv()
                gate = far_gate_of[b]
                joined[b, :, cols] = (
                    lift(gate, far_place[b, y], summed[block(b), :, cols], y)
                    + lift(gate, far_place[b, mate], via[b, :, cols], mate)).astype(BF16)
                outward(b, h).start()

    for h in range(PARTS):
        cols = pl.ds(h * tile, tile)
        total[:, cols] = inc[:, cols].astype(F32) + lift(gate_of[...], place_t[y], back[y, :, cols], y)

    for h in range(PARTS):
        cols = pl.ds(h * tile, tile)
        pltpu.make_async_remote_copy(
            summed.at[0, :, cols], back.at[mate, :, cols], ret_s.at[0, h], ret_r.at[h],
            device_id=at_row(mate), device_id_type=MESH).wait_recv()
        total[:, cols] = total[:, cols] + lift(gate_of[...], place_t[mate], back[mate, :, cols], mate)

    for h in range(PARTS):
        cols = pl.ds(h * tile, tile)
        outward(0, h).wait_recv()
        out[:, cols] = (total[:, cols] + given_in[:, cols].astype(F32)).astype(out.dtype)

    for copy in meta:
        copy.wait_send()

    for i in range(SHIFT_PARTS):
        shift(i, nxt).wait_send()

    @pl.when(enters)
    def _():
        for i in range(SHIFT_PARTS):
            second_leg(i).wait_send()

    for copy in narrow:
        copy.wait_send()
    for h in range(PARTS):
        wide(h).wait_send()
    for k in range(3):
        dispatch(k).wait_send()
    for i in range(4):
        relay(i).wait_send()
        for h in range(PARTS):
            partial(i, h).wait_send()
    for h in range(PARTS):
        giveback(mate, h).wait_send()
        for b in range(2):
            @pl.when(inner)
            def _():
                outward(b, h).wait_send()

            @pl.when(jnp.logical_not(inner))
            def _():
                inward(b, h).wait_send()


def local(acts, routes, gates, norm_gain, gate_w, up_w, down_w):
    tok, dim = acts.shape[1:]
    width = gate_w.shape[2]
    hbm = pl.BlockSpec(memory_space=pl.ANY)
    vmem = pl.BlockSpec(memory_space=pltpu.VMEM)
    dma = pltpu.SemaphoreType.DMA
    result = pl.pallas_call(
        kernel,
        name="relay_experts",
        out_shape=jax.ShapeDtypeStruct((tok, dim), BF16),
        in_specs=[hbm, vmem, vmem, vmem, hbm, hbm, hbm],
        out_specs=vmem,
        scratch_shapes=[
            pltpu.VMEM((tok, dim), BF16),
            pltpu.VMEM((tok, dim), BF16),
            pltpu.VMEM((3, CAP, dim), BF16),
            pltpu.VMEM((2, 4, CAP, dim), BF16),
            pltpu.VMEM((2, dim, width), BF16),
            pltpu.VMEM((2, dim, width), BF16),
            pltpu.VMEM((2 * width, dim), BF16),
            pltpu.VMEM((4, CAP, dim), BF16),
            pltpu.VMEM((CAP, dim), BF16),
            pltpu.VMEM((4, CAP, 2 * width), BF16),
            pltpu.VMEM((4, CAP, 2 * width), BF16),
            pltpu.VMEM((4, CAP, dim), F32),
            pltpu.VMEM((4, CAP, dim), BF16),
            pltpu.VMEM((4, CAP, dim), BF16),
            pltpu.VMEM((4, CAP, dim), BF16),
            pltpu.VMEM((4, CAP, dim), BF16),
            pltpu.VMEM((2, CAP, dim), BF16),
            pltpu.VMEM((2, tok, dim), BF16),
            pltpu.VMEM((tok, dim), BF16),
            pltpu.VMEM((tok, dim), F32),
            pltpu.VMEM((4, tok, tok), BF16),
            pltpu.VMEM((4, tok, tok), BF16),
            pltpu.VMEM((tok, tok), F32),
            pltpu.VMEM((2, 2, tok), jnp.int32),
            pltpu.VMEM((2, 2, tok), F32),
            pltpu.VMEM((2, 4, tok, tok), BF16),
            pltpu.VMEM((2, tok, tok), F32),
            dma((SHIFT_PARTS,)), dma((SHIFT_PARTS,)),
            dma((SHIFT_PARTS,)), dma((SHIFT_PARTS,)),
            dma((2 + PARTS,)), dma((2 + PARTS,)), dma((3,)),
            dma((3,)), dma((4,)),
            dma((4,)), dma((4,)),
            dma((4, PARTS)), dma((4, PARTS)),
            dma((4, PARTS)), dma((PARTS,)),
            dma((2, PARTS)), dma((2, PARTS)), dma((PARTS,)), dma((2,)), dma((2, 2)),
        ],
        compiler_params=pltpu.CompilerParams(
            collective_id=0, has_side_effects=True, vmem_limit_bytes=56 * 1024 * 1024),
    )(acts[0], routes[0].T, gates[0].T, norm_gain, gate_w[0], up_w[0], down_w[0])
    return result.reshape(1, tok, dim)


def solution(mesh):
    in_specs = (
        P("section", "expert", None),
        P("section", "expert", None),
        P("section", "expert", None),
        P("section", None),
        P("section", None, "expert"),
        P("section", None, "expert"),
        P("section", "expert", None),
    )
    out_specs = P("section", "expert", None)
    return jax.shard_map(local, mesh=mesh, in_specs=in_specs, out_specs=out_specs, check_vma=False)
```

```python
import functools

import jax
import jax.numpy as jnp
from jax import lax
from jax.experimental import pallas as pl
from jax.experimental.pallas import tpu as pltpu
from jax.sharding import PartitionSpec as P

NEXP = 4
CAP = 96
SHIFT_PARTS = 4
EARLY = 1
SOON = 2
PARTS = 2
PAIR = 1
LAG = 2
JOIN = 2
MESH = pl.DeviceIdType.MESH
F32 = jnp.float32
BF16 = jnp.bfloat16


def far_order(y, k):
    low = y < 2
    yy = jnp.where(low, y, 3 - y)
    d = 3 - k
    d = jnp.where(d <= yy, d - 1, d)
    return jnp.where(low, d, 3 - d)


def kernel(
    acts, routes, gates, gain, gate_w, up_w, down_w, out,
    inc, hop, packs, rows, wg, wu, wd, normed, mate_normed, hidden, mate_hidden, own_part, mate_part, got_part,
    summed, back, via, joined, given_in, total, place_t, place, gate_of, far_routes, far_gates, far_place, far_gate_of,
    shift_s, shift_r, hop_s, hop_r, w_s, w_r, w_l, y_s, y_r, rel_s, rel_r, part_s, part_r, ret_s, ret_r,
    via_r, join_s, join_r, meta_s, meta_r,
):
    tok, dim = inc.shape
    width = gate_w.shape[1]
    n_sec = lax.axis_size("section")
    half = n_sec // 2
    s = lax.axis_index("section")
    e = lax.axis_index("expert")
    core = lax.rem(s, 2)
    x = lax.rem(e, 4)
    y = e // 4
    flip = x + 1 - 2 * lax.rem(x, 2)
    cross = 3 - x
    wx = jnp.where(core == 0, flip, cross)
    tx = jnp.where(core == 0, cross, flip)
    nxt = (lax.rem(s + 1, n_sec), e)
    prv = (lax.rem(s + n_sec - 1, n_sec), e)
    wmate = (s, y * 4 + wx)
    tmate = (s, y * 4 + tx)
    leaves = lax.rem(s, half) == half - 1
    enters = lax.rem(s, half) == 0
    ring = (s // half) * 4 + y

    def around(steps, last):
        to = lax.rem(ring + 8 + steps, 8)
        return ((to // 4) * half + last * (half - 1), lax.rem(to, 4) * 4 + x)

    def at_row(r):
        return (s, r * 4 + x)

    def greet(peer):
        pl.semaphore_signal(barrier, inc=1, device_id=peer, device_id_type=MESH)

    barrier = pltpu.get_barrier_semaphore()
    greet(wmate)
    greet(tmate)
    for i in range(1, 4):
        greet(at_row(lax.rem(y + i, 4)))

    @pl.when(enters)
    def _():
        for last in range(2):
            greet(around(2, last))
            greet(around(-2, last))

    @pl.when(jnp.logical_not(enters))
    def _():
        greet(prv)

    local = [
        pltpu.make_async_copy(gate_w, wg.at[0], w_l.at[0]),
        pltpu.make_async_copy(up_w, wu.at[0], w_l.at[1]),
        pltpu.make_async_copy(down_w, wd.at[pl.ds(0, width)], w_l.at[2]),
    ]
    for copy in local:
        copy.start()
    pl.semaphore_wait(barrier, 6 + jnp.where(leaves, 1, 0) + jnp.where(enters, 2, 0))

    part = dim // SHIFT_PARTS
    columns = [pl.ds(i * part, part) for i in range(SHIFT_PARTS)]

    def shift(i, peer):
        return pltpu.make_async_remote_copy(
            acts.at[:, columns[i]], inc.at[:, columns[i]],
            shift_s.at[i], shift_r.at[i], device_id=peer, device_id_type=MESH)

    def first_leg(i):
        return pltpu.make_async_remote_copy(
            acts.at[:, columns[i]], hop.at[:, columns[i]], shift_s.at[i], hop_r.at[i],
            device_id=around(2 if i % 2 == 0 else -2, 0), device_id_type=MESH)

    def second_leg(i):
        return pltpu.make_async_remote_copy(
            hop.at[:, columns[i]], inc.at[:, columns[i]], hop_s.at[i], shift_r.at[i],
            device_id=around(2 if i % 2 == 0 else -2, 0), device_id_type=MESH)

    @pl.when(leaves)
    def _():
        for i in range(SHIFT_PARTS):
            first_leg(i).start()

    @pl.when(jnp.logical_not(leaves))
    def _():
        for i in range(SHIFT_PARTS):
            shift(i, nxt).start()

    tile = dim // PARTS
    narrow = [
        pltpu.make_async_remote_copy(src, dst.at[1], w_s.at[i], w_r.at[i], device_id=wmate, device_id_type=MESH)
        for i, (src, dst) in enumerate(((gate_w, wg), (up_w, wu)))
    ]

    def columns_of(h):
        return pl.ds(pl.multiple_of(h * tile, tile), tile)

    def wide(h):
        return pltpu.make_async_remote_copy(
            down_w.at[:, columns_of(h)], wd.at[pl.ds(width, width), columns_of(h)], w_s.at[2 + h], w_r.at[2 + h],
            device_id=wmate, device_id_type=MESH)

    for copy in narrow:
        copy.start()
    for h in range(PARTS):
        wide(h).start()

    inner = (y == 1) | (y == 2)
    mate = y + 1 - 2 * lax.rem(y, 2)
    across = jnp.where(y < 2, 2, 1)
    mine = jnp.where(inner, 1, 0)
    meta = [
        pltpu.make_async_remote_copy(
            src, dst.at[mine], meta_s.at[i], meta_r.at[mine, i], device_id=at_row(across), device_id_type=MESH)
        for i, (src, dst) in enumerate(((routes, far_routes), (gates, far_gates)))
    ]
    for copy in meta:
        copy.start()

    lane = lax.broadcasted_iota(jnp.int32, (tok, tok), 1)
    sub = lax.broadcasted_iota(jnp.int32, (tok, tok), 0)
    slot = sub.astype(F32)

    def table(ids, weights):
        first, second = ids[0:1, :] == sub, ids[1:2, :] == sub
        member = (first | second).astype(F32)
        gate = jnp.where(first, weights[0:1, :], 0.0) + jnp.where(second, weights[1:2, :], 0.0)
        rank = jnp.dot(member.astype(BF16), (sub <= lane).astype(BF16), preferred_element_type=F32) - 1.0
        hots = [jnp.where(rank[g:g + 1, :] == slot, member[g:g + 1, :], 0.0) for g in range(NEXP)]
        return gate.T, hots

    gate_of[...], hots = table(routes[...], gates[...])
    for g in range(NEXP):
        place[g] = hots[g].astype(BF16)
        place_t[g] = hots[g].T.astype(BF16)

    @pl.when(enters)
    def _():
        for i in range(SHIFT_PARTS):
            first_leg(i).wait_recv()
            second_leg(i).start()

    def packed(g, cols):
        return jnp.dot(place[g][:CAP], inc[:, cols], preferred_element_type=F32).astype(BF16)

    def dispatch(k, i):
        return pltpu.make_async_remote_copy(
            packs.at[k, :, columns[i]], rows.at[0, y, :, columns[i]], y_s.at[k, i], y_r.at[y],
            device_id=at_row(far_order(y, k)), device_id_type=MESH)

    for i in range(SHIFT_PARTS):
        shift(i, nxt).wait_recv()
        cols = columns[i]
        for k in range(3):
            packs[k, :, cols] = packed(far_order(y, k), cols)
            dispatch(k, i).start()
        rows[0, y, :, cols] = packed(y, cols)

    @pl.when(inner)
    def _():
        for i in range(2):
            for j, (src, dst) in enumerate(((routes, far_routes), (gates, far_gates))):
                pltpu.make_async_remote_copy(
                    src, dst.at[i], meta_s.at[j], meta_r.at[i, j], device_id=at_row(across),
                    device_id_type=MESH).wait_recv()
            far_gate_of[i], far_hots = table(far_routes[i], far_gates[i])
            for g in range(NEXP):
                far_place[i, g] = far_hots[g].T.astype(BF16)

    def arrival(src):
        return pltpu.make_async_remote_copy(
            packs.at[0], rows.at[0, src], y_s.at[0, 0], y_r.at[src],
            device_id=at_row(src), device_id_type=MESH)

    def relay(src):
        return pltpu.make_async_remote_copy(
            rows.at[0, src], rows.at[1, src], rel_s.at[src], rel_r.at[src],
            device_id=tmate, device_id_type=MESH)

    def block(b):
        return jnp.where(b == 3, y, far_order(y, jnp.minimum(b, 2)))

    def norm(which, src):
        xf = rows[which, src].astype(F32)
        scale = lax.rsqrt(jnp.mean(xf * xf, axis=1, keepdims=True) + 1e-06)
        return (xf * scale * gain[...]).astype(BF16)

    def activate(xn, part):
        gpart = jnp.dot(xn, wg[part], preferred_element_type=F32)
        upart = jnp.dot(xn, wu[part], preferred_element_type=F32)
        return (jax.nn.silu(gpart) * upart).astype(BF16)

    @pl.when(enters)
    def _():
        relay(y).start()

    normed[y] = norm(0, y)

    @pl.loop(0, 3)
    def _(b):
        src = block(b)
        arrival(src).wait_recv()

        @pl.when((b < EARLY) | enters)
        def _():
            relay(src).start()

        normed[src] = norm(0, src)

    for copy in local:
        copy.wait()

    def own_rows(part):
        for pair in range(2):
            xn = normed[pl.ds(2 * pair, 2)].reshape(2 * CAP, dim)
            hidden[pl.ds(2 * pair, 2), :, pl.ds(part * width, width)] = activate(xn, part).reshape(2, CAP, width)

    own_rows(0)
    relay(block(0)).wait_recv()
    mate_normed[...] = norm(1, block(0))
    mate_hidden[block(0), :, pl.ds(0, width)] = activate(mate_normed[...], 0)
    narrow[0].wait_recv()

    @pl.when(jnp.logical_not(enters))
    def _():
        for b in range(EARLY, SOON):
            relay(block(b)).start()

    narrow[1].wait_recv()

    def partial(src, h):
        return pltpu.make_async_remote_copy(
            mate_part.at[src, :, columns_of(h)], got_part.at[src, :, columns_of(h)], part_s.at[src, h], part_r.at[src, h],
            device_id=tmate, device_id_type=MESH)

    def giveback(src, h):
        return pltpu.make_async_remote_copy(
            summed.at[src, :, columns_of(h)], back.at[y, :, columns_of(h)], ret_s.at[src, h], ret_r.at[h],
            device_id=at_row(mate), device_id_type=MESH)

    def inward(b, h):
        return pltpu.make_async_remote_copy(
            summed.at[block(b), :, columns_of(h)], via.at[b, :, columns_of(h)], ret_s.at[block(b), h], via_r.at[b, h],
            device_id=at_row(mate), device_id_type=MESH)

    def outward(b, h):
        return pltpu.make_async_remote_copy(
            joined.at[b, :, columns_of(h)], given_in.at[:, columns_of(h)], join_s.at[b, h], join_r.at[h],
            device_id=at_row(block(b)), device_id_type=MESH)

    def lift(gate, hot, value, g):
        gate = jnp.sum(jnp.where(lane == g, gate, 0.0), axis=1, keepdims=True)
        return gate * jnp.dot(hot[:, :CAP], value, preferred_element_type=F32)

    def item(i):
        i = jnp.maximum(i, 0)
        j = lax.rem(i, PAIR * PARTS)
        return i // (PAIR * PARTS) * PAIR + lax.rem(j, PAIR), j // PAIR

    @pl.loop(0, 4 * PARTS + LAG + JOIN)
    def _(i):
        @pl.when(i < 4 * PARTS)
        def _():
            b, h = item(i)
            src = block(b)
            cols = columns_of(h)

            @pl.when((h == 0) & (b > 0))
            def _():
                relay(src).wait_recv()
                mate_normed[...] = norm(1, src)
                mate_hidden[src, :, pl.ds(0, width)] = activate(mate_normed[...], 0)

            @pl.when(h == 0)
            def _():
                mate_hidden[src, :, pl.ds(width, width)] = activate(mate_normed[...], 1)

            @pl.when(b == 0)
            def _():
                wide(h).wait_recv()

            mate_part[src, :, cols] = jnp.dot(
                mate_hidden[src], wd[:, cols], preferred_element_type=F32).astype(BF16)
            partial(src, h).start()

            @pl.when((h == 0) & (b + SOON < 4) & jnp.logical_not(enters))
            def _():
                relay(block(b + SOON)).start()

            @pl.when(i == 0)
            def _():
                own_rows(1)

            own_part[src, :, cols] = jnp.dot(hidden[src], wd[:, cols], preferred_element_type=F32)

        @pl.when((i >= LAG) & (i < 4 * PARTS + LAG))
        def _():
            b, h = item(i - LAG)
            src = block(b)
            cols = columns_of(h)
            partial(src, h).wait_recv()
            value = (own_part[src, :, cols] + got_part[src, :, cols].astype(F32)).astype(BF16)

            @pl.when(b < 3)
            def _():
                summed[src, :, cols] = value

            @pl.when((b < 2) & jnp.logical_not(inner))
            def _():
                inward(b, h).start()

            @pl.when(b == 2)
            def _():
                giveback(src, h).start()

            @pl.when(b == 3)
            def _():
                back[y, :, cols] = value

        @pl.when(inner & (i >= LAG + JOIN))
        def _():
            b, h = item(i - LAG - JOIN)

            @pl.when(b < 2)
            def _():
                cols = columns_of(h)
                inward(b, h).wait_recv()
                gate = far_gate_of[b]
                joined[b, :, cols] = (
                    lift(gate, far_place[b, y], summed[block(b), :, cols], y)
                    + lift(gate, far_place[b, mate], via[b, :, cols], mate)).astype(BF16)
                outward(b, h).start()

    for h in range(PARTS):
        cols = pl.ds(h * tile, tile)
        total[:, cols] = inc[:, cols].astype(F32) + lift(gate_of[...], place_t[y], back[y, :, cols], y)

    for h in range(PARTS):
        cols = pl.ds(h * tile, tile)
        pltpu.make_async_remote_copy(
            summed.at[0, :, cols], back.at[mate, :, cols], ret_s.at[0, h], ret_r.at[h],
            device_id=at_row(mate), device_id_type=MESH).wait_recv()
        total[:, cols] = total[:, cols] + lift(gate_of[...], place_t[mate], back[mate, :, cols], mate)

    for h in range(PARTS):
        cols = pl.ds(h * tile, tile)
        outward(0, h).wait_recv()
        out[:, cols] = (total[:, cols] + given_in[:, cols].astype(F32)).astype(out.dtype)

    for copy in meta:
        copy.wait_send()

    for i in range(SHIFT_PARTS):
        shift(i, nxt).wait_send()

    @pl.when(enters)
    def _():
        for i in range(SHIFT_PARTS):
            second_leg(i).wait_send()

    for copy in narrow:
        copy.wait_send()
    for h in range(PARTS):
        wide(h).wait_send()
    for k in range(3):
        for i in range(SHIFT_PARTS):
            dispatch(k, i).wait_send()
    for i in range(4):
        relay(i).wait_send()
        for h in range(PARTS):
            partial(i, h).wait_send()
    for h in range(PARTS):
        giveback(mate, h).wait_send()
        for b in range(2):
            @pl.when(inner)
            def _():
                outward(b, h).wait_send()

            @pl.when(jnp.logical_not(inner))
            def _():
                inward(b, h).wait_send()


def local(acts, routes, gates, norm_gain, gate_w, up_w, down_w):
    tok, dim = acts.shape[1:]
    width = gate_w.shape[2]
    hbm = pl.BlockSpec(memory_space=pl.ANY)
    vmem = pl.BlockSpec(memory_space=pltpu.VMEM)
    dma = pltpu.SemaphoreType.DMA
    result = pl.pallas_call(
        kernel,
        name="relay_experts",
        out_shape=jax.ShapeDtypeStruct((tok, dim), BF16),
        in_specs=[hbm, vmem, vmem, vmem, hbm, hbm, hbm],
        out_specs=vmem,
        scratch_shapes=[
            pltpu.VMEM((tok, dim), BF16),
            pltpu.VMEM((tok, dim), BF16),
            pltpu.VMEM((3, CAP, dim), BF16),
            pltpu.VMEM((2, 4, CAP, dim), BF16),
            pltpu.VMEM((2, dim, width), BF16),
            pltpu.VMEM((2, dim, width), BF16),
            pltpu.VMEM((2 * width, dim), BF16),
            pltpu.VMEM((4, CAP, dim), BF16),
            pltpu.VMEM((CAP, dim), BF16),
            pltpu.VMEM((4, CAP, 2 * width), BF16),
            pltpu.VMEM((4, CAP, 2 * width), BF16),
            pltpu.VMEM((4, CAP, dim), F32),
            pltpu.VMEM((4, CAP, dim), BF16),
            pltpu.VMEM((4, CAP, dim), BF16),
            pltpu.VMEM((4, CAP, dim), BF16),
            pltpu.VMEM((4, CAP, dim), BF16),
            pltpu.VMEM((2, CAP, dim), BF16),
            pltpu.VMEM((2, tok, dim), BF16),
            pltpu.VMEM((tok, dim), BF16),
            pltpu.VMEM((tok, dim), F32),
            pltpu.VMEM((4, tok, tok), BF16),
            pltpu.VMEM((4, tok, tok), BF16),
            pltpu.VMEM((tok, tok), F32),
            pltpu.VMEM((2, 2, tok), jnp.int32),
            pltpu.VMEM((2, 2, tok), F32),
            pltpu.VMEM((2, 4, tok, tok), BF16),
            pltpu.VMEM((2, tok, tok), F32),
            dma((SHIFT_PARTS,)), dma((SHIFT_PARTS,)),
            dma((SHIFT_PARTS,)), dma((SHIFT_PARTS,)),
            dma((2 + PARTS,)), dma((2 + PARTS,)), dma((3,)),
            dma((3, SHIFT_PARTS)), dma((4,)),
            dma((4,)), dma((4,)),
            dma((4, PARTS)), dma((4, PARTS)),
            dma((4, PARTS)), dma((PARTS,)),
            dma((2, PARTS)), dma((2, PARTS)), dma((PARTS,)), dma((2,)), dma((2, 2)),
        ],
        compiler_params=pltpu.CompilerParams(
            collective_id=0, has_side_effects=True, vmem_limit_bytes=56 * 1024 * 1024),
    )(acts[0], routes[0].T, gates[0].T, norm_gain, gate_w[0], up_w[0], down_w[0])
    return result.reshape(1, tok, dim)


def solution(mesh):
    in_specs = (
        P("section", "expert", None),
        P("section", "expert", None),
        P("section", "expert", None),
        P("section", None),
        P("section", None, "expert"),
        P("section", None, "expert"),
        P("section", "expert", None),
    )
    out_specs = P("section", "expert", None)
    return jax.shard_map(local, mesh=mesh, in_specs=in_specs, out_specs=out_specs, check_vma=False)
```
